128 devices in a mesh: subj: 8 (over x, y_lo), slab: 16 (over y_hi, z, core).
Axes of the slice: x: 4, y: 4 (y_hi: 2, y_lo: 2; y = y_hi * 2 + y_lo), z: 4, core: 2. Of those that a mesh axis runs over, the one named last changes fastest.
Arguments:
- subjects: float32 [16, 128, 448, 128], P('subj', 'slab'), may hold values from -8 to 8
- templates: float32 [4, 128, 448, 128], P(None, 'slab', 'subj'), may hold values from -6 to 6
- labels: int32 [16], replicated, may hold values from 0 to 3, as said below
- group_live_counts: int32 [8], replicated, may hold values from 1 to 2, as said below
Outputs:
- new_templates: float32 [4, 128, 448, 128], P(None, 'slab', 'subj')
The draws below stay inside these ranges and needn't reach their ends.
Inputs may be any that keep to these rules, and one draw needn't show every extreme that they name: `labels`: slot j belongs to group j // 2; slot 0 of group g has label g mod 4. The live slots of group g are its first group_live_counts[g] slots; the other slots hold volumes of no subject; some group has all 2 slots live.
All inputs are finite; a program needn't handle non-finite values.
Results may differ from the reference program's by a relative error of at most 0.00002.
Values sent between devices are 32-bit elements; how exact they have to be, the bound alone decides.
No kernel may reach another device: no remote copies, remote signals or barrier semaphores. Data moves between devices by JAX's collectives and lax.ppermute only.
A program may use at most 192 MiB of HBM per device.

```python
import jax
import jax.numpy as jnp
from jax import lax

TEMPLATE_COUNT = 4
RADIUS = 4
GROUP_SLOTS = 2
X = 448
Y = 128
Z = 128
GROUPS = 8
SUBJECTS = 16


def label_field(key):
    base_key = jax.random.fold_in(key, 11)
    drawn = jax.random.randint(base_key, (SUBJECTS,), 0, TEMPLATE_COUNT, dtype=jnp.int32)
    slot_positions = jnp.arange(SUBJECTS, dtype=jnp.int32)
    forced = slot_positions // GROUP_SLOTS % TEMPLATE_COUNT
    return jnp.where(slot_positions % GROUP_SLOTS == 0, forced, drawn).astype(jnp.int32)


def template_field(key):
    base_key = jax.random.fold_in(key, 23)
    return jnp.clip(jax.random.normal(base_key, (TEMPLATE_COUNT, Z, X, Y), jnp.float32), -6.0, 6.0)


def draw_templates(key, part):
    return template_field(key)


def draw_labels(key, part):
    return label_field(key)


def draw_subjects(key, part):
    cluster_ids = label_field(key)
    base_templates = template_field(key)
    gains = jax.random.uniform(jax.random.fold_in(key, 31), (SUBJECTS,), jnp.float32, 0.6, 1.4)
    noise = 0.5 * jax.random.normal(jax.random.fold_in(key, 37), (SUBJECTS, Z, X, Y), jnp.float32)
    mixed = gains[:, None, None, None] * base_templates[cluster_ids] + noise
    return jnp.clip(mixed, -8.0, 8.0)


def draw_group_live_counts(key, part):
    base_key = jax.random.fold_in(key, 41)
    first_draw = jax.random.randint(jax.random.fold_in(base_key, 1), (GROUPS,), 0, GROUP_SLOTS, dtype=jnp.int32)
    second_draw = jax.random.randint(jax.random.fold_in(base_key, 2), (GROUPS,), 0, GROUP_SLOTS, dtype=jnp.int32)
    counts = 1 + first_draw * second_draw // max(GROUP_SLOTS - 1, 1)
    busiest = jax.random.randint(jax.random.fold_in(base_key, 3), (), 0, GROUPS, dtype=jnp.int32)
    return jnp.where(jnp.arange(GROUPS, dtype=jnp.int32) == busiest, GROUP_SLOTS, counts).astype(jnp.int32)


def setup_inputs(seed: int = 0) -> dict:
    streams_of = jax.random.split(jax.random.key(seed), 5)
    subjects = draw_subjects(jax.random.fold_in(streams_of[4], 71), 0)
    templates = draw_templates(jax.random.fold_in(streams_of[4], 71), 0)
    labels = draw_labels(jax.random.fold_in(streams_of[4], 71), 0)
    group_live_counts = draw_group_live_counts(jax.random.fold_in(streams_of[4], 71), 0)
    return {"subjects": subjects, "templates": templates, "labels": labels, "group_live_counts": group_live_counts}


epsilon = 1e-5
step_size = 0.5


def window_sum(volume, which_axis, extent):
    running = lax.slice_in_dim(volume, 0, extent, axis=which_axis)
    for offset in range(1, 2 * RADIUS + 1):
        running = running + lax.slice_in_dim(volume, offset, offset + extent, axis=which_axis)
    return running


def padded_sum(volume, which_axis):
    widths = [(0, 0)] * volume.ndim
    widths[which_axis] = (RADIUS, RADIUS)
    return window_sum(jnp.pad(volume, widths), which_axis, volume.shape[which_axis])


def plane_box(volume, leading):
    return padded_sum(padded_sum(volume, leading), leading + 1)


def similarity_gradient(subject, template):
    window = float((2 * RADIUS + 1) ** 3)
    channels = jnp.stack([subject, template, subject * subject, template * template, subject * template])
    local_sums = plane_box(padded_sum(channels, 1), 2)
    subject_sum = local_sums[0]
    template_sum = local_sums[1]
    covariance = local_sums[4] - subject_sum * template_sum / window
    subject_variance = local_sums[2] - subject_sum * subject_sum / window
    template_variance = local_sums[3] - template_sum * template_sum / window
    denominator = subject_variance * template_variance + epsilon
    cross_weight = 2.0 * covariance / denominator
    spread_weight = -covariance * covariance * subject_variance / (denominator * denominator)
    mean_weight = -(cross_weight * subject_sum + 2.0 * spread_weight * template_sum) / window
    stacked = jnp.stack([mean_weight, cross_weight, spread_weight])
    filtered = plane_box(padded_sum(stacked, 1), 2)
    return filtered[0] + filtered[1] * subject + 2.0 * filtered[2] * template


def reference(subjects, templates, labels, group_live_counts):
    slot_positions = jnp.arange(SUBJECTS, dtype=jnp.int32)
    live_mask = ((slot_positions % GROUP_SLOTS) < group_live_counts[slot_positions // GROUP_SLOTS]).astype(jnp.float32)
    cluster_membership = (labels[:, None] == jnp.arange(TEMPLATE_COUNT, dtype=jnp.int32)[None, :]).astype(jnp.float32) * live_mask[:, None]
    members = jnp.sum(cluster_membership, axis=0)

    def accumulate(slot_number, cluster_totals):
        cluster_label = labels[slot_number]
        subject = lax.dynamic_index_in_dim(subjects, slot_number, 0, keepdims=False)
        template = lax.dynamic_index_in_dim(templates, cluster_label, 0, keepdims=False)
        template_gradient = similarity_gradient(subject, template)
        return cluster_totals.at[cluster_label].add(live_mask[slot_number] * template_gradient)

    cluster_totals = lax.fori_loop(0, SUBJECTS, accumulate, jnp.zeros(templates.shape, jnp.float32))
    return templates + step_size * cluster_totals / members[:, None, None, None]
```

```python
import functools

import jax
import jax.numpy as jnp
from jax import lax
from jax.experimental import pallas as pl
from jax.experimental.pallas import tpu as pltpu
from jax.sharding import PartitionSpec as P

RADIUS = 4
RIM = 2 * RADIUS
WINDOW = 2 * RADIUS + 1
INVERSE = 1.0 / float(WINDOW**3)
ROWS = 8
epsilon = 1e-05


def neighbours(block, axis):
    low, high = block
    count = lax.axis_size(axis)
    forward = [(i, i + 1) for i in range(count - 1)]
    backward = [(target, source) for source, target in forward]
    return lax.ppermute(high, axis, forward), lax.ppermute(low, axis, backward)


def window(planes):
    count = len(planes)
    outputs = count - WINDOW + 1
    prefix, suffix = list(planes), list(planes)
    for i in range(count):
        if i % WINDOW:
            prefix[i] = prefix[i - 1] + planes[i]
    for i in reversed(range(min(outputs - outputs % WINDOW + WINDOW, count) - 1)):
        if i % WINDOW == 0 and i + WINDOW <= count:
            suffix[i] = prefix[i + WINDOW - 1]
        elif i % WINDOW < WINDOW - 1:
            suffix[i] = suffix[i + 1] + planes[i]
    return [
        suffix[i] if i % WINDOW == 0 else suffix[i] + prefix[i + WINDOW - 1]
        for i in range(outputs)
    ]


def y_box(values, band_ref):
    high = values.astype(jnp.bfloat16)
    rest = values - high.astype(jnp.float32)
    middle = rest.astype(jnp.bfloat16)
    low = (rest - middle.astype(jnp.float32)).astype(jnp.bfloat16)
    both = jnp.concatenate([high, middle], axis=1)
    return jnp.dot(both, band_ref[...], preferred_element_type=jnp.float32) + jnp.dot(
        low, band_ref[: values.shape[1]], preferred_element_type=jnp.float32
    )


def zy_box(channels, columns, band_ref, out_ref):
    def step(i, carry):
        rows = pl.ds(pl.multiple_of(i * ROWS, ROWS), ROWS)
        for c, planes in enumerate(channels(rows)):
            sums = window(planes)
            boxed = y_box(jnp.concatenate(sums, axis=0), band_ref)
            for z in range(len(sums)):
                out_ref[c, z, rows, :] = boxed[z * ROWS : (z + 1) * ROWS]
        return carry

    lax.fori_loop(0, columns, step, 0)


def x_box(ref, c, z, count):
    total = ref[c, z, pl.ds(0, count), :]
    for d in range(1, WINDOW):
        total = total + ref[c, z, pl.ds(d, count), :]
    return total


def layers(refs, index, rows):
    depth = refs[0].shape[1]
    return [ref[index, z, rows, :] for ref in refs for z in range(depth)]


def template_kernel(before, own, after, band, mean_ref, var_ref, work):
    def channels(rows):
        planes = layers((before, own, after), 0, rows)
        return planes, [v * v for v in planes]

    zy_box(channels, own.shape[2] // ROWS, band, work)

    def step(z, carry):
        total = x_box(work, 0, z, mean_ref.shape[2])
        mean = total * INVERSE
        mean_ref[0, z] = mean
        var_ref[0, z] = x_box(work, 1, z, mean_ref.shape[2]) - total * mean
        return carry

    lax.fori_loop(0, mean_ref.shape[1], step, 0)


def slot_kernel(
    first, scalars, before, own, after, t_before, t_own, t_after, mean_t, var_t, band, *rest
):
    starts, rest = ([], rest) if first else (rest[:3], rest[3:])
    sum_a, sum_q, sum_p, work, coef, boxed = rest
    slot = pl.program_id(0)
    count = pl.num_programs(0)

    @pl.when(slot == 0)
    def _():
        if first:
            for ref in (sum_a, sum_q, sum_p):
                ref[...] = jnp.zeros_like(ref)
        else:
            for ref, start in zip((sum_a, sum_q, sum_p), starts):
                ref[...] = start[...]

    @pl.when(scalars[count + slot] != 0)
    def _():
        label = scalars[slot]
        x_low, x_high, z_low, z_high = (scalars[2 * count + i] for i in range(4))

        def channels(rows):
            s = layers((before, own, after), 0, rows)
            t = layers((t_before, t_own, t_after), label, rows)
            return s, [v * v for v in s], [v * w for v, w in zip(s, t)]

        zy_box(channels, own.shape[2] // ROWS, band, work)
        width = coef.shape[2]
        row = lax.broadcasted_iota(jnp.int32, (width, own.shape[3]), 0)

        def middle(z, carry):
            inside = (z >= z_low) & (z < z_high)
            low = jnp.where(inside, x_low, width)
            s_sum = x_box(work, 0, z, width)
            s_mean = s_sum * INVERSE
            s_var = x_box(work, 1, z, width) - s_sum * s_mean
            t_mean = mean_t[label, z]
            covariance = x_box(work, 2, z, width) - s_sum * t_mean
            weight = covariance / (s_var * var_t[label, z] + epsilon)
            weight = jnp.where((row >= low) & (row < x_high), weight, 0.0)
            spread = weight * s_var
            coef[0, z] = weight
            sum_a[label, z] += weight * (s_mean - spread * t_mean)
            sum_q[label, z] += weight * spread
            return carry

        lax.fori_loop(0, coef.shape[1], middle, 0)

        def weights(rows):
            return ([coef[0, z, rows, :] for z in range(coef.shape[1])],)

        zy_box(weights, width // ROWS, band, boxed)

        def close(z, carry):
            centre = own[0, z, RIM : own.shape[2] - RIM, :]
            sum_p[label, z] += x_box(boxed, 0, z, sum_p.shape[2]) * centre
            return carry

        lax.fori_loop(0, sum_p.shape[1], close, 0)


def close_kernel(scale, sum_a, sum_q, sum_p, t_own, band, out_ref, boxed):
    k = pl.program_id(0)

    def channels(rows):
        return [[ref[0, z, rows, :] for z in range(ref.shape[1])] for ref in (sum_a, sum_q)]

    zy_box(channels, sum_a.shape[2] // ROWS, band, boxed)

    def step(z, carry):
        t = t_own[0, z, RIM : t_own.shape[2] - RIM, :]
        width = out_ref.shape[2]
        total = sum_p[0, z] - x_box(boxed, 0, z, width) - x_box(boxed, 1, z, width) * t
        out_ref[0, z] = t + total * scale[k]
        return carry

    lax.fori_loop(0, out_ref.shape[1], step, 0)


def per_device(subjects, templates, labels, group_live_counts):
    slots, depth, length, lanes = subjects.shape
    clusters, _, extent, _ = templates.shape
    groups = group_live_counts.shape[0]
    padded = extent + 2 * RIM
    middle_depth, middle_extent = depth + RIM, extent + RIM
    group_index = lax.axis_index("subj")
    slab_index = lax.axis_index("slab")

    own_labels = labels.reshape(groups, slots)
    live = jnp.arange(slots, dtype=jnp.int32)[None, :] < group_live_counts[:, None]
    members = jnp.sum(
        (own_labels[:, :, None] == jnp.arange(clusters, dtype=jnp.int32)) & live[:, :, None],
        axis=(0, 1),
    ).astype(jnp.float32)
    bounds = jnp.stack(
        [
            jnp.where(group_index == 0, RADIUS, 0),
            jnp.where(group_index == groups - 1, middle_extent - RADIUS, middle_extent),
            jnp.where(slab_index == 0, RADIUS, 0),
            jnp.where(slab_index == lax.axis_size("slab") - 1, middle_depth - RADIUS, middle_depth),
        ]
    ).astype(jnp.int32)

    reach = jnp.abs(jnp.arange(lanes)[:, None] - jnp.arange(lanes)[None, :]) <= RADIUS
    band = jnp.concatenate([reach, reach], axis=0).astype(jnp.bfloat16)

    low, high = neighbours((templates[:, :, :RIM], templates[:, :, extent - RIM :]), "subj")
    t_own = jnp.concatenate([low, templates, high], axis=2)
    t_before, t_after = neighbours((t_own, t_own), "slab")

    wide = jnp.pad(subjects, ((0, 0), (0, 0), (RIM, RIM), (0, 0)))
    pieces = []
    for j in range(slots):
        chunks = jnp.stack([wide[j, :, g * extent : g * extent + padded] for g in range(groups)])
        own = lax.all_to_all(chunks, "subj", 0, 0, tiled=True)
        before, after = neighbours((own, own), "slab")
        pieces.append((before, own, after))

    def block(shape):
        return pl.BlockSpec((1,) + shape, lambda i, *_: (i,) + (0,) * len(shape))

    def whole(shape):
        return pl.BlockSpec(shape, lambda i, *_: (0,) * len(shape), pipeline_mode=pl.Buffered(1))

    t_block = (depth, padded, lanes)
    m_block = (middle_depth, middle_extent, lanes)
    o_block = (depth, extent, lanes)
    f32 = functools.partial(jax.ShapeDtypeStruct, dtype=jnp.float32)
    params = pltpu.CompilerParams(vmem_limit_bytes=60 * 1024 * 1024)

    def cost(count, size):
        return pl.CostEstimate(flops=count, bytes_accessed=size, transcendentals=0)

    mean_t, var_t = pl.pallas_call(
        template_kernel,
        grid=(clusters,),
        in_specs=[block(t_block)] * 3 + [whole(band.shape)],
        out_specs=[block(m_block)] * 2,
        out_shape=[f32((clusters,) + m_block)] * 2,
        scratch_shapes=[pltpu.VMEM((2, middle_depth, padded, lanes), jnp.float32)],
        compiler_params=params,
        cost_estimate=cost(1 << 28, 1 << 23),
        name="templates",
    )(t_before, t_own, t_after, band)

    sums = ()
    sum_shapes = [(clusters,) + m_block] * 2 + [(clusters,) + o_block]
    for j in range(slots):
        scalars = jnp.concatenate([own_labels[:, j], live[:, j].astype(jnp.int32), bounds])
        sums = pl.pallas_call(
            functools.partial(slot_kernel, j == 0),
            grid_spec=pltpu.PrefetchScalarGridSpec(
                num_scalar_prefetch=1,
                grid=(groups,),
                in_specs=[block(t_block)] * 3
                + [whole((clusters,) + t_block)] * 3
                + [whole((clusters,) + m_block)] * 2
                + [whole(band.shape)]
                + [whole(s.shape) for s in sums],
                out_specs=[whole(s) for s in sum_shapes],
                scratch_shapes=[
                    pltpu.VMEM((3, middle_depth, padded, lanes), jnp.float32),
                    pltpu.VMEM((1,) + m_block, jnp.float32),
                    pltpu.VMEM((1, depth, middle_extent, lanes), jnp.float32),
                ],
            ),
            out_shape=[f32(s) for s in sum_shapes],
            compiler_params=params,
            cost_estimate=cost(1 << 30, 1 << 25),
            name=f"slots_{j}",
        )(scalars, *pieces[j], t_before, t_own, t_after, mean_t, var_t, band, *sums)

    return pl.pallas_call(
        close_kernel,
        grid=(clusters,),
        in_specs=[pl.BlockSpec(memory_space=pltpu.SMEM)]
        + [block(m_block)] * 2
        + [block(o_block), block(t_block), whole(band.shape)],
        out_specs=block(o_block),
        out_shape=f32((clusters,) + o_block),
        scratch_shapes=[pltpu.VMEM((2, depth, middle_extent, lanes), jnp.float32)],
        compiler_params=params,
        cost_estimate=cost(1 << 28, 1 << 23),
        name="close",
    )(1.0 / members, *sums, t_own, band)


def solution(mesh):
    in_specs = (P("subj", "slab", None, None), P(None, "slab", "subj", None), P(), P())
    out_specs = P(None, "slab", "subj", None)
    return jax.shard_map(
        per_device, mesh=mesh, in_specs=in_specs, out_specs=out_specs, check_vma=False
    )
```

```python
import functools

import jax
import jax.numpy as jnp
from jax import lax
from jax.experimental import pallas as pl
from jax.experimental.pallas import tpu as pltpu
from jax.sharding import PartitionSpec as P

RADIUS = 4
RIM = 2 * RADIUS
WINDOW = 2 * RADIUS + 1
INVERSE = 1.0 / float(WINDOW**3)
ROWS = 8
epsilon = 1e-05


def neighbours(block, axis):
    low, high = block
    count = lax.axis_size(axis)
    forward = [(i, i + 1) for i in range(count - 1)]
    backward = [(target, source) for source, target in forward]
    return lax.ppermute(high, axis, forward), lax.ppermute(low, axis, backward)


def window(planes):
    count = len(planes)
    outputs = count - WINDOW + 1
    prefix, suffix = list(planes), list(planes)
    for i in range(count):
        if i % WINDOW:
            prefix[i] = prefix[i - 1] + planes[i]
    for i in reversed(range(min(outputs - outputs % WINDOW + WINDOW, count) - 1)):
        if i % WINDOW == 0 and i + WINDOW <= count:
            suffix[i] = prefix[i + WINDOW - 1]
        elif i % WINDOW < WINDOW - 1:
            suffix[i] = suffix[i + 1] + planes[i]
    return [
        suffix[i] if i % WINDOW == 0 else suffix[i] + prefix[i + WINDOW - 1]
        for i in range(outputs)
    ]


def y_box(values, band_ref):
    high = values.astype(jnp.bfloat16)
    rest = (values - high.astype(jnp.float32)).astype(jnp.bfloat16)
    return jnp.dot(
        jnp.concatenate([high, rest], axis=1), band_ref[...], preferred_element_type=jnp.float32
    )


def zy_box(channels, columns, band_ref, out_ref, unroll):
    def step(i, carry):
        sums, places = [], []
        for j in range(unroll):
            rows = pl.ds(pl.multiple_of((i * unroll + j) * ROWS, ROWS), ROWS)
            for c, planes in enumerate(channels(rows)):
                boxes = window(planes)
                sums += boxes
                places += [(c, z, rows) for z in range(len(boxes))]
        boxed = y_box(jnp.concatenate(sums, axis=0), band_ref)
        for k, (c, z, rows) in enumerate(places):
            out_ref[c, z, rows, :] = boxed[k * ROWS : (k + 1) * ROWS]
        return carry

    lax.fori_loop(0, columns // unroll, step, 0)


def x_box(ref, c, z, count, work, slot):
    third = RADIUS - 1
    wide = count + 2 * RADIUS
    work[slot, :wide] = sum_of([ref[c, z, pl.ds(d, wide), :] for d in range(third)])
    return sum_of([work[slot, pl.ds(d * third, count), :] for d in range(third)])


def sum_of(values):
    return functools.reduce(lambda a, b: a + b, values)


def layers(refs, index, rows):
    depth = refs[0].shape[1]
    return [ref[index, z, rows, :] for ref in refs for z in range(depth)]


def template_kernel(before, own, after, band, mean_ref, var_ref, work, thirds):
    def channels(rows):
        planes = layers((before, own, after), 0, rows)
        return planes, [v * v for v in planes]

    zy_box(channels, own.shape[2] // ROWS, band, work, 3)

    def step(z, carry):
        count = mean_ref.shape[2]
        total = x_box(work, 0, z, count, thirds, 0)
        mean = total * INVERSE
        mean_ref[0, z] = mean
        var_ref[0, z] = x_box(work, 1, z, count, thirds, 1) - total * mean
        return carry

    lax.fori_loop(0, mean_ref.shape[1], step, 0, unroll=2)


def clear_rim(ref, index, edges):
    depth, width = ref.shape[1], ref.shape[2]
    parts = (
        (slice(None), slice(0, RADIUS)),
        (slice(None), slice(width - RADIUS, width)),
        (slice(0, RADIUS), slice(None)),
        (slice(depth - RADIUS, depth), slice(None)),
    )
    for edge, (z, x) in zip(edges, parts):

        @pl.when(edge != 0)
        def _():
            part = ref[index, z, x, :]
            ref[index, z, x, :] = jnp.zeros_like(part)


def slot_kernel(
    first, scalars, before, own, after, t_before, t_own, t_after, mean_t, var_t, band, *rest
):
    if first:
        sum_a, sum_q, sum_p, work, thirds, coef, boxed = rest
    else:
        scale, *starts, out_ref, sum_a, sum_q, sum_p, work, thirds, coef, boxed = rest
    slot = pl.program_id(0)
    count = pl.num_programs(0)
    edges = [scalars[2 * count + i] for i in range(4)]

    @pl.when(slot == 0)
    def _():
        if first:
            for ref in (sum_a, sum_q, sum_p):
                ref[...] = jnp.zeros_like(ref)
        else:
            for ref, start in zip((sum_a, sum_q, sum_p), starts):
                pltpu.sync_copy(start, ref)

    @pl.when(scalars[count + slot] != 0)
    def _():
        label = scalars[slot]

        def channels(rows):
            s = layers((before, own, after), 0, rows)
            t = layers((t_before, t_own, t_after), label, rows)
            return s, [v * v for v in s], [v * w for v, w in zip(s, t)]

        zy_box(channels, own.shape[2] // ROWS, band, work, 3)
        width = coef.shape[2]

        def middle(z, carry):
            s_sum = x_box(work, 0, z, width, thirds, 0)
            s_var = x_box(work, 1, z, width, thirds, 1) - s_sum * (s_sum * INVERSE)
            t_mean = mean_t[label, z]
            covariance = x_box(work, 2, z, width, thirds, 2) - s_sum * t_mean
            weight = covariance / (s_var * var_t[label, z] + epsilon)
            spread = weight * s_var
            coef[0, z] = weight
            sum_a[label, z] += weight * (s_sum * INVERSE - spread * t_mean)
            sum_q[label, z] += weight * spread
            return carry

        lax.fori_loop(0, coef.shape[1], middle, 0, unroll=2)
        clear_rim(coef, 0, edges)

        def weights(rows):
            return ([coef[0, z, rows, :] for z in range(coef.shape[1])],)

        zy_box(weights, width // ROWS, band, boxed, 4)

        def close(z, carry):
            centre = own[0, z, RIM : own.shape[2] - RIM, :]
            sum_p[label, z] += x_box(boxed, 0, z, sum_p.shape[2], thirds, 0) * centre
            return carry

        lax.fori_loop(0, sum_p.shape[1], close, 0, unroll=4)

    if first:
        return

    @pl.when(slot == count - 1)
    def _():
        def cluster(k, carry):
            clear_rim(sum_a, k, edges)
            clear_rim(sum_q, k, edges)

            def channels(rows):
                return [[ref[k, z, rows, :] for z in range(ref.shape[1])] for ref in (sum_a, sum_q)]

            zy_box(channels, sum_a.shape[2] // ROWS, band, work, 2)

            def step(z, carry):
                t = t_own[k, z, RIM : t_own.shape[2] - RIM, :]
                width = out_ref.shape[2]
                total = sum_p[k, z] - x_box(work, 0, z, width, thirds, 0)
                total = total - x_box(work, 1, z, width, thirds, 1) * t
                out_ref[k, z] = t + total * scale[k]
                return carry

            return lax.fori_loop(0, out_ref.shape[1], step, carry, unroll=2)

        lax.fori_loop(0, out_ref.shape[0], cluster, 0)


def per_device(subjects, templates, labels, group_live_counts):
    slots, depth, length, lanes = subjects.shape
    clusters, _, extent, _ = templates.shape
    groups = group_live_counts.shape[0]
    padded = extent + 2 * RIM
    middle_depth, middle_extent = depth + RIM, extent + RIM
    group_index = lax.axis_index("subj")
    slab_index = lax.axis_index("slab")

    own_labels = labels.reshape(groups, slots)
    live = jnp.arange(slots, dtype=jnp.int32)[None, :] < group_live_counts[:, None]
    members = jnp.sum(
        (own_labels[:, :, None] == jnp.arange(clusters, dtype=jnp.int32)) & live[:, :, None],
        axis=(0, 1),
    ).astype(jnp.float32)
    edges = jnp.stack(
        [
            group_index == 0,
            group_index == groups - 1,
            slab_index == 0,
            slab_index == lax.axis_size("slab") - 1,
        ]
    ).astype(jnp.int32)

    reach = jnp.abs(jnp.arange(lanes)[:, None] - jnp.arange(lanes)[None, :]) <= RADIUS
    band = jnp.concatenate([reach, reach], axis=0).astype(jnp.bfloat16)

    low, high = neighbours((templates[:, :, :RIM], templates[:, :, extent - RIM :]), "subj")
    t_own = jnp.concatenate([low, templates, high], axis=2)

    def chunks_of(part):
        wide = jnp.pad(part, ((0, 0), (RIM, RIM), (0, 0)))
        return jnp.stack([wide[:, g * extent : g * extent + padded] for g in range(groups)])

    def exchange(chunks):
        return lax.all_to_all(chunks, "subj", 0, 0, tiled=True)

    chunks, t_own = lax.optimization_barrier((chunks_of(subjects[0]), t_own))
    t_before, t_after = neighbours((t_own, t_own), "slab")
    own = exchange(chunks)
    part, t_before, t_after = lax.optimization_barrier((subjects[1], t_before, t_after))
    next_chunks = chunks_of(part)

    def block(shape):
        return pl.BlockSpec((1,) + shape, lambda i, *_: (i,) + (0,) * len(shape))

    def whole(shape):
        return pl.BlockSpec(shape, lambda i, *_: (0,) * len(shape), pipeline_mode=pl.Buffered(1))

    t_block = (depth, padded, lanes)
    m_block = (middle_depth, middle_extent, lanes)
    o_block = (depth, extent, lanes)
    f32 = functools.partial(jax.ShapeDtypeStruct, dtype=jnp.float32)
    params = pltpu.CompilerParams(vmem_limit_bytes=60 * 1024 * 1024)

    def cost(count, size):
        return pl.CostEstimate(flops=count, bytes_accessed=size, transcendentals=0)

    spare = padded + ROWS
    mean_t, var_t = pl.pallas_call(
        template_kernel,
        grid=(clusters,),
        in_specs=[block(t_block)] * 3 + [whole(band.shape)],
        out_specs=[block(m_block)] * 2,
        out_shape=[f32((clusters,) + m_block)] * 2,
        scratch_shapes=[
            pltpu.VMEM((2, middle_depth, spare, lanes), jnp.float32),
            pltpu.VMEM((2, spare, lanes), jnp.float32),
        ],
        compiler_params=params,
        cost_estimate=cost(1 << 28, 1 << 23),
        name="templates",
    )(t_before, t_own, t_after, band)

    own, next_chunks, mean_t = lax.optimization_barrier((own, next_chunks, mean_t))
    before, after = neighbours((own, own), "slab")
    next_own = exchange(next_chunks)
    next_before, next_after = neighbours((next_own, next_own), "slab")
    (own, before, after), next_own = lax.optimization_barrier(((own, before, after), next_own))
    pieces = [(before, own, after), (next_before, next_own, next_after)]

    sum_shapes = [(clusters,) + m_block] * 2 + [(clusters,) + o_block]
    work_shapes = [
        pltpu.VMEM((3, middle_depth, spare, lanes), jnp.float32),
        pltpu.VMEM((3, spare, lanes), jnp.float32),
        pltpu.VMEM((1,) + m_block, jnp.float32),
        pltpu.VMEM((1, depth, spare, lanes), jnp.float32),
    ]

    def slots_call(j, extra, extra_specs, out_shapes, scratch):
        scalars = jnp.concatenate([own_labels[:, j], live[:, j].astype(jnp.int32), edges])
        return pl.pallas_call(
            functools.partial(slot_kernel, j == 0),
            grid_spec=pltpu.PrefetchScalarGridSpec(
                num_scalar_prefetch=1,
                grid=(groups,),
                in_specs=[block(t_block)] * 3
                + [whole((clusters,) + t_block)] * 3
                + [whole((clusters,) + m_block)] * 2
                + [whole(band.shape)]
                + extra_specs,
                out_specs=[whole(s) for s in out_shapes],
                scratch_shapes=scratch + work_shapes,
            ),
            out_shape=[f32(s) for s in out_shapes],
            compiler_params=params,
            cost_estimate=cost(1 << 30, 1 << 25),
            name=f"slots_{j}",
        )(scalars, *pieces[j], t_before, t_own, t_after, mean_t, var_t, band, *extra)

    sums = slots_call(0, [], [], sum_shapes, [])
    return slots_call(
        1,
        [1.0 / members, *sums],
        [pl.BlockSpec(memory_space=pltpu.SMEM)] + [pl.BlockSpec(memory_space=pl.ANY)] * 3,
        [(clusters,) + o_block],
        [pltpu.VMEM(s, jnp.float32) for s in sum_shapes],
    )[0]


def solution(mesh):
    in_specs = (P("subj", "slab", None, None), P(None, "slab", "subj", None), P(), P())
    out_specs = P(None, "slab", "subj", None)
    return jax.shard_map(
        per_device, mesh=mesh, in_specs=in_specs, out_specs=out_specs, check_vma=False
    )
```

```python
import functools

import jax
import jax.numpy as jnp
from jax import lax
from jax.experimental import pallas as pl
from jax.experimental.pallas import tpu as pltpu
from jax.sharding import PartitionSpec as P

RADIUS = 4
RIM = 2 * RADIUS
WINDOW = 2 * RADIUS + 1
INVERSE = 1.0 / float(WINDOW**3)
ROWS = 8
epsilon = 1e-05


def neighbours(block, axis):
    low, high = block
    count = lax.axis_size(axis)
    forward = [(i, i + 1) for i in range(count - 1)]
    backward = [(target, source) for source, target in forward]
    return lax.ppermute(high, axis, forward), lax.ppermute(low, axis, backward)


def window(planes):
    count = len(planes)
    outputs = count - WINDOW + 1
    prefix, suffix = list(planes), list(planes)
    for i in range(count):
        if i % WINDOW:
            prefix[i] = prefix[i - 1] + planes[i]
    for i in reversed(range(min(outputs - outputs % WINDOW + WINDOW, count) - 1)):
        if i % WINDOW == 0 and i + WINDOW <= count:
            suffix[i] = prefix[i + WINDOW - 1]
        elif i % WINDOW < WINDOW - 1:
            suffix[i] = suffix[i + 1] + planes[i]
    return [
        suffix[i] if i % WINDOW == 0 else suffix[i] + prefix[i + WINDOW - 1]
        for i in range(outputs)
    ]


def y_box(values, band_ref):
    high = values.astype(jnp.bfloat16)
    rest = (values - high.astype(jnp.float32)).astype(jnp.bfloat16)
    return jnp.dot(
        jnp.concatenate([high, rest], axis=1), band_ref[...], preferred_element_type=jnp.float32
    )


def zy_box(channels, columns, band_ref, out_ref, unroll):
    def step(i, carry):
        sums, places = [], []
        for j in range(unroll):
            rows = pl.ds(pl.multiple_of((i * unroll + j) * ROWS, ROWS), ROWS)
            for c, planes in enumerate(channels(rows)):
                boxes = window(planes)
                sums += boxes
                places += [(c, z, rows) for z in range(len(boxes))]
        boxed = y_box(jnp.concatenate(sums, axis=0), band_ref)
        for k, (c, z, rows) in enumerate(places):
            out_ref[c, z, rows, :] = boxed[k * ROWS : (k + 1) * ROWS]
        return carry

    lax.fori_loop(0, columns // unroll, step, 0)


def x_box(ref, c, z, count, work, slot):
    third = RADIUS - 1
    wide = count + 2 * RADIUS
    work[slot, :wide] = sum_of([ref[c, z, pl.ds(d, wide), :] for d in range(third)])
    return sum_of([work[slot, pl.ds(d * third, count), :] for d in range(third)])


def sum_of(values):
    return functools.reduce(lambda a, b: a + b, values)


def layers(refs, index, rows):
    depth = refs[0].shape[1]
    return [ref[index, z, rows, :] for ref in refs for z in range(depth)]


def template_kernel(before, own, after, band, mean_ref, var_ref, work, thirds):
    def channels(rows):
        planes = layers((before, own, after), 0, rows)
        return planes, [v * v for v in planes]

    zy_box(channels, own.shape[2] // ROWS, band, work, 3)

    def step(z, carry):
        count = mean_ref.shape[2]
        total = x_box(work, 0, z, count, thirds, 0)
        mean = total * INVERSE
        mean_ref[0, z] = mean
        var_ref[0, z] = x_box(work, 1, z, count, thirds, 1) - total * mean
        return carry

    lax.fori_loop(0, mean_ref.shape[1], step, 0, unroll=2)


def clear_rim(ref, index, edges):
    depth, width = ref.shape[1], ref.shape[2]
    parts = (
        (slice(None), slice(0, RADIUS)),
        (slice(None), slice(width - RADIUS, width)),
        (slice(0, RADIUS), slice(None)),
        (slice(depth - RADIUS, depth), slice(None)),
    )
    for edge, (z, x) in zip(edges, parts):

        @pl.when(edge != 0)
        def _():
            part = ref[index, z, x, :]
            ref[index, z, x, :] = jnp.zeros_like(part)


def pick_kernel(scalars, source, out_ref):
    out_ref[...] = source[...]


def slot_kernel(first, groups, scalars, before, own, after, *rest):
    if first:
        sources, rest = rest[:5], rest[5:]
        band, sum_a, sum_q, sum_p, *rest = rest
        targets, rest = rest[:5], rest[5:]
    else:
        scale, *rest = rest
        sources, rest = rest[:8], rest[8:]
        band, out_ref, *rest = rest
        targets, rest = rest[:8], rest[8:]
        sum_a, sum_q, sum_p = targets[5:]
    t_before, t_own, t_after, mean_t, var_t = targets[:5]
    work, thirds, coef, boxed, sems = rest
    step_index = pl.program_id(0)
    live_count = scalars[3 * groups]
    edges = [scalars[3 * groups + 1 + i] for i in range(4)]
    label = scalars[2 * groups + step_index]
    copies = [
        pltpu.make_async_copy(source, target, sems.at[i])
        for i, (source, target) in enumerate(zip(sources, targets))
    ]

    @pl.when(step_index == 0)
    def _():
        for copy in copies:
            copy.start()
        if first:
            for ref in (sum_a, sum_q, sum_p):
                ref[...] = jnp.zeros_like(ref)
        for copy in copies[:3]:
            copy.wait()

    @pl.when(step_index < live_count)
    def _():
        def channels(rows):
            s = layers((before, own, after), 0, rows)
            t = layers((t_before, t_own, t_after), label, rows)
            return s, [v * v for v in s], [v * w for v, w in zip(s, t)]

        zy_box(channels, own.shape[2] // ROWS, band, work, 3)

    @pl.when(step_index == 0)
    def _():
        for copy in copies[3:]:
            copy.wait()

    @pl.when(step_index < live_count)
    def _():
        width = coef.shape[2]

        def middle(z, carry):
            s_sum = x_box(work, 0, z, width, thirds, 0)
            s_var = x_box(work, 1, z, width, thirds, 1) - s_sum * (s_sum * INVERSE)
            t_mean = mean_t[label, z]
            covariance = x_box(work, 2, z, width, thirds, 2) - s_sum * t_mean
            weight = covariance / (s_var * var_t[label, z] + epsilon)
            spread = weight * s_var
            coef[0, z] = weight
            sum_a[label, z] += weight * (s_sum * INVERSE - spread * t_mean)
            sum_q[label, z] += weight * spread
            return carry

        lax.fori_loop(0, coef.shape[1], middle, 0, unroll=4)
        clear_rim(coef, 0, edges)

        def weights(rows):
            return ([coef[0, z, rows, :] for z in range(coef.shape[1])],)

        zy_box(weights, width // ROWS, band, boxed, 4)

        def close(z, carry):
            centre = own[0, z, RIM : own.shape[2] - RIM, :]
            sum_p[label, z] += x_box(boxed, 0, z, sum_p.shape[2], thirds, 0) * centre
            return carry

        lax.fori_loop(0, sum_p.shape[1], close, 0, unroll=4)

    if first:
        return

    @pl.when(step_index == pl.num_programs(0) - 1)
    def _():
        def cluster(k, carry):
            clear_rim(sum_a, k, edges)
            clear_rim(sum_q, k, edges)

            def channels(rows):
                return [[ref[k, z, rows, :] for z in range(ref.shape[1])] for ref in (sum_a, sum_q)]

            zy_box(channels, sum_a.shape[2] // ROWS, band, work, 4)

            def step(z, carry):
                t = t_own[k, z, RIM : t_own.shape[2] - RIM, :]
                width = out_ref.shape[2]
                total = sum_p[k, z] - x_box(work, 0, z, width, thirds, 0)
                total = total - x_box(work, 1, z, width, thirds, 1) * t
                out_ref[k, z] = t + total * scale[k]
                return carry

            return lax.fori_loop(0, out_ref.shape[1], step, carry, unroll=4)

        lax.fori_loop(0, out_ref.shape[0], cluster, 0)


def per_device(subjects, templates, labels, group_live_counts):
    slots, depth, length, lanes = subjects.shape
    clusters, _, extent, _ = templates.shape
    groups = group_live_counts.shape[0]
    padded = extent + 2 * RIM
    middle_depth, middle_extent = depth + RIM, extent + RIM
    group_index = lax.axis_index("subj")
    slab_index = lax.axis_index("slab")

    own_labels = labels.reshape(groups, slots)
    live = jnp.arange(slots, dtype=jnp.int32)[None, :] < group_live_counts[:, None]
    members = jnp.sum(
        (own_labels[:, :, None] == jnp.arange(clusters, dtype=jnp.int32)) & live[:, :, None],
        axis=(0, 1),
    ).astype(jnp.float32)
    edges = jnp.stack(
        [
            group_index == 0,
            group_index == groups - 1,
            slab_index == 0,
            slab_index == lax.axis_size("slab") - 1,
        ]
    ).astype(jnp.int32)

    reach = jnp.abs(jnp.arange(lanes)[:, None] - jnp.arange(lanes)[None, :]) <= RADIUS
    band = jnp.concatenate([reach, reach], axis=0).astype(jnp.bfloat16)

    def chunks_of(part):
        wide = jnp.pad(part, ((0, 0), (RIM, RIM), (0, 0)))
        return jnp.stack([wide[:, g * extent : g * extent + padded] for g in range(groups)])

    def exchange(chunks):
        return lax.all_to_all(chunks, "subj", 0, 0, tiled=True)

    chunks, templates = lax.optimization_barrier((chunks_of(subjects[0]), templates))
    with jax.named_scope("swap_0"):
        own = exchange(chunks)

    with jax.named_scope("rim_x"):
        low, high = neighbours((templates[:, :, :RIM], templates[:, :, extent - RIM :]), "subj")
    t_own = jnp.concatenate([low, templates, high], axis=2)
    next_chunks = chunks_of(subjects[1])

    def block(shape):
        return pl.BlockSpec((1,) + shape, lambda i, *_: (i,) + (0,) * len(shape))

    def whole(shape):
        return pl.BlockSpec(shape, lambda i, *_: (0,) * len(shape), pipeline_mode=pl.Buffered(1))

    t_block = (depth, padded, lanes)
    m_block = (middle_depth, middle_extent, lanes)
    o_block = (depth, extent, lanes)
    f32 = functools.partial(jax.ShapeDtypeStruct, dtype=jnp.float32)
    params = pltpu.CompilerParams(vmem_limit_bytes=60 * 1024 * 1024)

    def cost(count, size):
        return pl.CostEstimate(flops=count, bytes_accessed=size, transcendentals=0)

    own, next_chunks, t_own = lax.optimization_barrier((own, next_chunks, t_own))
    with jax.named_scope("depth_0"):
        before, after = neighbours((own, own), "slab")
    with jax.named_scope("rim_z"):
        t_before, t_after = neighbours((t_own, t_own), "slab")
    with jax.named_scope("swap_1"):
        next_own = exchange(next_chunks)

    spare = padded + ROWS
    mean_t, var_t = pl.pallas_call(
        template_kernel,
        grid=(clusters,),
        in_specs=[block(t_block)] * 3 + [whole(band.shape)],
        out_specs=[block(m_block)] * 2,
        out_shape=[f32((clusters,) + m_block)] * 2,
        scratch_shapes=[
            pltpu.VMEM((2, middle_depth, spare, lanes), jnp.float32),
            pltpu.VMEM((2, spare, lanes), jnp.float32),
        ],
        compiler_params=params,
        cost_estimate=cost(1 << 28, 1 << 23),
        name="templates",
    )(t_before, t_own, t_after, band)

    second = live[:, 1]
    live_count = jnp.sum(second).astype(jnp.int32)
    index = jnp.arange(groups, dtype=jnp.int32)
    earlier = jnp.sum((index[None, :] < index[:, None]) & second[None, :], axis=1)
    ranks = jnp.where(second, earlier, groups)
    place = jnp.minimum(index, jnp.maximum(live_count - 1, 0))
    found = ranks[None, :] == place[:, None]
    order = jnp.sum(jnp.where(found, index[None, :], 0), axis=1)
    labels_in_order = jnp.sum(jnp.where(found, own_labels[:, 1][None, :], 0), axis=1)
    counted = jnp.full((1,), groups, jnp.int32)
    scalars = (
        jnp.concatenate([index, index, own_labels[:, 0], counted, edges]),
        jnp.concatenate([order, place, labels_in_order, live_count[None], edges]),
    )

    sum_shapes = [(clusters,) + m_block] * 2 + [(clusters,) + o_block]
    big = [t_before, t_own, t_after, mean_t, var_t]
    anywhere = pl.BlockSpec(memory_space=pl.ANY)

    def in_order(shape, offset):
        return pl.BlockSpec(
            (1,) + shape, lambda i, table: (table[offset + i],) + (0,) * len(shape)
        )

    def slots_call(j, steps, pieces, extra):
        first = j == 0
        sources = big + ([] if first else list(extra))
        return pl.pallas_call(
            functools.partial(slot_kernel, first, groups),
            grid_spec=pltpu.PrefetchScalarGridSpec(
                num_scalar_prefetch=1,
                grid=(steps,),
                in_specs=[in_order(t_block, offset) for offset in (groups, 0, groups)]
                + ([] if first else [pl.BlockSpec(memory_space=pltpu.SMEM)])
                + [anywhere] * len(sources)
                + [whole(band.shape)],
                out_specs=[whole(s) for s in (sum_shapes if first else [(clusters,) + o_block])],
                scratch_shapes=[pltpu.VMEM(s.shape, jnp.float32) for s in sources]
                + [
                    pltpu.VMEM((3, middle_depth, spare, lanes), jnp.float32),
                    pltpu.VMEM((3, spare, lanes), jnp.float32),
                    pltpu.VMEM((1,) + m_block, jnp.float32),
                    pltpu.VMEM((1, depth, spare, lanes), jnp.float32),
                    pltpu.SemaphoreType.DMA((len(sources),)),
                ],
            ),
            out_shape=[f32(s) for s in (sum_shapes if first else [(clusters,) + o_block])],
            compiler_params=params,
            cost_estimate=cost(steps << 27, 1 << 25),
            name=f"slots_{j}",
        )(scalars[j], *pieces, *([] if first else [1.0 / members]), *sources, band)

    def pick(steps):
        return pl.pallas_call(
            pick_kernel,
            grid_spec=pltpu.PrefetchScalarGridSpec(
                num_scalar_prefetch=1,
                grid=(steps,),
                in_specs=[in_order(t_block, 0)],
                out_specs=pl.BlockSpec((1,) + t_block, lambda i, table: (i, 0, 0, 0)),
            ),
            out_shape=f32((steps,) + t_block),
            compiler_params=params,
            cost_estimate=cost(1 << 20, steps << 20),
            name="pick",
        )(scalars[1], next_own)

    def finish(steps):
        def branch():
            picked = pick(steps)
            with jax.named_scope("depth_1"):
                next_before, next_after = neighbours((picked, picked), "slab")
            sums = slots_call(0, groups, (before, own, after), ())
            return slots_call(1, steps, (next_before, next_own, next_after), sums)[0]

        return branch

    sizes = (2, 4, groups)
    which = sum((live_count > size).astype(jnp.int32) for size in sizes[:-1])
    return lax.switch(which, [finish(size) for size in sizes])


def solution(mesh):
    in_specs = (P("subj", "slab", None, None), P(None, "slab", "subj", None), P(), P())
    out_specs = P(None, "slab", "subj", None)
    return jax.shard_map(
        per_device, mesh=mesh, in_specs=in_specs, out_specs=out_specs, check_vma=False
    )
```

```python
import functools

import jax
import jax.numpy as jnp
from jax import lax
from jax.experimental import pallas as pl
from jax.experimental.pallas import tpu as pltpu
from jax.sharding import PartitionSpec as P

RADIUS = 4
RIM = 2 * RADIUS
WINDOW = 2 * RADIUS + 1
INVERSE = 1.0 / float(WINDOW**3)
ROWS = 8
epsilon = 1e-05


def neighbours(block, axis):
    low, high = block
    count = lax.axis_size(axis)
    forward = [(i, i + 1) for i in range(count - 1)]
    backward = [(target, source) for source, target in forward]
    return lax.ppermute(high, axis, forward), lax.ppermute(low, axis, backward)


def window(planes):
    count = len(planes)
    outputs = count - WINDOW + 1
    prefix, suffix = list(planes), list(planes)
    for i in range(count):
        if i % WINDOW:
            prefix[i] = prefix[i - 1] + planes[i]
    for i in reversed(range(min(outputs - outputs % WINDOW + WINDOW, count) - 1)):
        if i % WINDOW == 0 and i + WINDOW <= count:
            suffix[i] = prefix[i + WINDOW - 1]
        elif i % WINDOW < WINDOW - 1:
            suffix[i] = suffix[i + 1] + planes[i]
    return [
        suffix[i] if i % WINDOW == 0 else suffix[i] + prefix[i + WINDOW - 1]
        for i in range(outputs)
    ]


def y_box(values, band_ref):
    high = values.astype(jnp.bfloat16)
    rest = (values - high.astype(jnp.float32)).astype(jnp.bfloat16)
    return jnp.dot(
        jnp.concatenate([high, rest], axis=1), band_ref[...], preferred_element_type=jnp.float32
    )


def zy_box(channels, columns, band_ref, out_ref, unroll):
    def step(i, carry):
        sums, places = [], []
        for j in range(unroll):
            rows = pl.ds(pl.multiple_of((i * unroll + j) * ROWS, ROWS), ROWS)
            for c, planes in enumerate(channels(rows)):
                boxes = window(planes)
                sums += boxes
                places += [(c, z, rows) for z in range(len(boxes))]
        boxed = y_box(jnp.concatenate(sums, axis=0), band_ref)
        for k, (c, z, rows) in enumerate(places):
            out_ref[c, z, rows, :] = boxed[k * ROWS : (k + 1) * ROWS]
        return carry

    lax.fori_loop(0, columns // unroll, step, 0)


def x_box(ref, c, z, count, work, slot):
    third = RADIUS - 1
    wide = count + 2 * RADIUS
    work[slot, :wide] = sum_of([ref[c, z, pl.ds(d, wide), :] for d in range(third)])
    return sum_of([work[slot, pl.ds(d * third, count), :] for d in range(third)])


def sum_of(values):
    return functools.reduce(lambda a, b: a + b, values)


def layers(refs, index, rows):
    depth = refs[0].shape[1]
    return [ref[index, z, rows, :] for ref in refs for z in range(depth)]


def template_kernel(before, own, after, band, mean_ref, var_ref, work, thirds):
    def channels(rows):
        planes = layers((before, own, after), 0, rows)
        return planes, [v * v for v in planes]

    zy_box(channels, own.shape[2] // ROWS, band, work, 3)

    def step(z, carry):
        count = mean_ref.shape[2]
        total = x_box(work, 0, z, count, thirds, 0)
        mean = total * INVERSE
        mean_ref[0, z] = mean
        var_ref[0, z] = x_box(work, 1, z, count, thirds, 1) - total * mean
        return carry

    lax.fori_loop(0, mean_ref.shape[1], step, 0, unroll=2)


def clear_rim(ref, index, edges):
    depth, width = ref.shape[1], ref.shape[2]
    parts = (
        (slice(None), slice(0, RADIUS)),
        (slice(None), slice(width - RADIUS, width)),
        (slice(0, RADIUS), slice(None)),
        (slice(depth - RADIUS, depth), slice(None)),
    )
    for edge, (z, x) in zip(edges, parts):

        @pl.when(edge != 0)
        def _():
            part = ref[index, z, x, :]
            ref[index, z, x, :] = jnp.zeros_like(part)


def pick_kernel(scalars, source, out_ref):
    out_ref[...] = source[...]


def chunk_kernel(source, out_ref):
    g = pl.program_id(0)
    last = pl.num_programs(0) - 1
    padded = out_ref.shape[2]
    extent = padded - 2 * RIM
    length = source.shape[2]

    @pl.when(g == 0)
    def _():
        out_ref[0, :, :RIM, :] = jnp.zeros_like(out_ref[0, :, :RIM, :])
        out_ref[0, :, RIM:, :] = source[0, :, : padded - RIM, :]

    @pl.when(g == last)
    def _():
        out_ref[0, :, : padded - RIM, :] = source[0, :, length - padded + RIM :, :]
        out_ref[0, :, padded - RIM :, :] = jnp.zeros_like(out_ref[0, :, padded - RIM :, :])

    @pl.when((g > 0) & (g < last))
    def _():
        start = pl.multiple_of(g * extent - RIM, ROWS)
        out_ref[0] = source[0, :, pl.ds(start, padded), :]


def slot_kernel(first, last, steps, scalars, before, own, after, *rest):
    scale = None
    if last:
        scale, *rest = rest
    count = 3 if first else 6
    sources, rest = rest[:count], rest[count:]
    band, *rest = rest
    if last:
        out_ref, *rest = rest
        targets, rest = rest[:6], rest[6:]
        sum_a, sum_q, sum_p = targets[3:]
    else:
        sum_a, sum_q, sum_p, *rest = rest
        targets, rest = list(rest[:3]) + ([] if first else [sum_a, sum_q, sum_p]), rest[3:]
    t_all, mean_t, var_t = targets[:3]
    clusters = mean_t.shape[0]
    work, thirds, coef, boxed, sems = rest
    step_index = pl.program_id(0)
    live_count = scalars[3 * steps]
    edges = [scalars[3 * steps + 1 + i] for i in range(4)]
    label = scalars[2 * steps + step_index]
    copies = [
        pltpu.make_async_copy(source, target, sems.at[i])
        for i, (source, target) in enumerate(zip(sources, targets))
    ]

    @pl.when(step_index == 0)
    def _():
        for copy in copies:
            copy.start()
        if first:
            for ref in (sum_a, sum_q, sum_p):
                ref[...] = jnp.zeros_like(ref)
        copies[0].wait()

    @pl.when(step_index < live_count)
    def _():
        def channels(rows):
            s = layers((before, own, after), 0, rows)
            t = sum((layers((t_all,), label + k * clusters, rows) for k in range(3)), [])
            return s, [v * v for v in s], [v * w for v, w in zip(s, t)]

        zy_box(channels, own.shape[2] // ROWS, band, work, 3)

    @pl.when(step_index == 0)
    def _():
        for copy in copies[1:]:
            copy.wait()

    @pl.when(step_index < live_count)
    def _():
        width = coef.shape[2]

        def middle(z, carry):
            s_sum = x_box(work, 0, z, width, thirds, 0)
            s_var = x_box(work, 1, z, width, thirds, 1) - s_sum * (s_sum * INVERSE)
            t_mean = mean_t[label, z]
            covariance = x_box(work, 2, z, width, thirds, 2) - s_sum * t_mean
            weight = covariance / (s_var * var_t[label, z] + epsilon)
            spread = weight * s_var
            coef[0, z] = weight
            sum_a[label, z] += weight * (s_sum * INVERSE - spread * t_mean)
            sum_q[label, z] += weight * spread
            return carry

        lax.fori_loop(0, coef.shape[1], middle, 0, unroll=4)
        clear_rim(coef, 0, edges)

        def weights(rows):
            return ([coef[0, z, rows, :] for z in range(coef.shape[1])],)

        zy_box(weights, width // ROWS, band, boxed, 4)

        def close(z, carry):
            centre = own[0, z, RIM : own.shape[2] - RIM, :]
            sum_p[label, z] += x_box(boxed, 0, z, sum_p.shape[2], thirds, 0) * centre
            return carry

        lax.fori_loop(0, sum_p.shape[1], close, 0, unroll=4)

    if not last:
        return

    @pl.when(step_index == pl.num_programs(0) - 1)
    def _():
        def cluster(k, carry):
            clear_rim(sum_a, k, edges)
            clear_rim(sum_q, k, edges)

            def channels(rows):
                return [[ref[k, z, rows, :] for z in range(ref.shape[1])] for ref in (sum_a, sum_q)]

            zy_box(channels, sum_a.shape[2] // ROWS, band, work, 4)

            def step(z, carry):
                t = t_all[k + clusters, z, RIM : t_all.shape[2] - RIM, :]
                width = out_ref.shape[2]
                total = sum_p[k, z] - x_box(work, 0, z, width, thirds, 0)
                total = total - x_box(work, 1, z, width, thirds, 1) * t
                out_ref[k, z] = t + total * scale[k]
                return carry

            return lax.fori_loop(0, out_ref.shape[1], step, carry, unroll=4)

        lax.fori_loop(0, out_ref.shape[0], cluster, 0)


def per_device(subjects, templates, labels, group_live_counts):
    slots, depth, length, lanes = subjects.shape
    clusters, _, extent, _ = templates.shape
    groups = group_live_counts.shape[0]
    padded = extent + 2 * RIM
    middle_depth, middle_extent = depth + RIM, extent + RIM
    group_index = lax.axis_index("subj")
    slab_index = lax.axis_index("slab")

    own_labels = labels.reshape(groups, slots)
    live = jnp.arange(slots, dtype=jnp.int32)[None, :] < group_live_counts[:, None]
    members = jnp.sum(
        (own_labels[:, :, None] == jnp.arange(clusters, dtype=jnp.int32)) & live[:, :, None],
        axis=(0, 1),
    ).astype(jnp.float32)
    edges = jnp.stack(
        [
            group_index == 0,
            group_index == groups - 1,
            slab_index == 0,
            slab_index == lax.axis_size("slab") - 1,
        ]
    ).astype(jnp.int32)

    reach = jnp.abs(jnp.arange(lanes)[:, None] - jnp.arange(lanes)[None, :]) <= RADIUS
    band = jnp.concatenate([reach, reach], axis=0).astype(jnp.bfloat16)

    def block(shape):
        return pl.BlockSpec((1,) + shape, lambda i, *_: (i,) + (0,) * len(shape))

    def whole(shape):
        return pl.BlockSpec(shape, lambda i, *_: (0,) * len(shape), pipeline_mode=pl.Buffered(1))

    t_block = (depth, padded, lanes)
    m_block = (middle_depth, middle_extent, lanes)
    o_block = (depth, extent, lanes)
    spare = padded + ROWS
    f32 = functools.partial(jax.ShapeDtypeStruct, dtype=jnp.float32)
    params = pltpu.CompilerParams(vmem_limit_bytes=60 * 1024 * 1024)

    def cost(count, size):
        return pl.CostEstimate(flops=count, bytes_accessed=size, transcendentals=0)

    def chunks_of(j, volumes):
        return pl.pallas_call(
            chunk_kernel,
            grid=(groups,),
            in_specs=[
                pl.BlockSpec(
                    (1, depth, length, lanes), lambda i: (j, 0, 0, 0), pipeline_mode=pl.Buffered(1)
                )
            ],
            out_specs=block(t_block),
            out_shape=f32((groups,) + t_block),
            compiler_params=params,
            cost_estimate=cost(1 << 20, 1 << 22),
            name=f"chunks_{j}",
        )(volumes)

    def exchange(chunks):
        return lax.all_to_all(chunks, "subj", 0, 0, tiled=True)

    with jax.named_scope("rim_z"):
        below, above = neighbours((templates, templates), "slab")
    with jax.named_scope("swap_0"):
        own = exchange(chunks_of(0, subjects))

    stack = jnp.concatenate([below, templates, above], axis=0)
    with jax.named_scope("rim_x"):
        low, high = neighbours((stack[:, :, :RIM], stack[:, :, extent - RIM :]), "subj")
    t_all = jnp.concatenate([low, stack, high], axis=2)
    next_chunks = chunks_of(1, subjects)

    second = live[:, 1]
    live_count = jnp.sum(second).astype(jnp.int32)
    index = jnp.arange(groups, dtype=jnp.int32)
    earlier = jnp.sum((index[None, :] < index[:, None]) & second[None, :], axis=1)
    ranks = jnp.where(second, earlier, groups)
    place = jnp.minimum(index, jnp.maximum(live_count - 1, 0))
    found = ranks[None, :] == place[:, None]
    order = jnp.sum(jnp.where(found, index[None, :], 0), axis=1)
    labels_in_order = jnp.sum(jnp.where(found, own_labels[:, 1][None, :], 0), axis=1)

    def table(own_index, rim_index, chosen, count):
        return jnp.concatenate(
            [own_index, rim_index, chosen, jnp.full((1,), count, jnp.int32), edges]
        )

    sum_shapes = [(clusters,) + m_block] * 2 + [(clusters,) + o_block]
    anywhere = pl.BlockSpec(memory_space=pl.ANY)

    def in_order(shape, offset):
        return pl.BlockSpec(
            (1,) + shape, lambda i, values: (values[offset + i],) + (0,) * len(shape)
        )

    def slots_call(name, steps, values, pieces, sums, last):
        first = not sums
        sources = [t_all, mean_t, var_t, *sums]
        out_shapes = [(clusters,) + o_block] if last else sum_shapes
        scratch = sources if last else sources[:3]
        return pl.pallas_call(
            functools.partial(slot_kernel, first, last, steps),
            grid_spec=pltpu.PrefetchScalarGridSpec(
                num_scalar_prefetch=1,
                grid=(steps,),
                in_specs=[in_order(t_block, offset) for offset in (steps, 0, steps)]
                + ([pl.BlockSpec(memory_space=pltpu.SMEM)] if last else [])
                + [anywhere] * len(sources)
                + [whole(band.shape)],
                out_specs=[whole(s) for s in out_shapes],
                scratch_shapes=[pltpu.VMEM(s.shape, jnp.float32) for s in scratch]
                + [
                    pltpu.VMEM((3, middle_depth, spare, lanes), jnp.float32),
                    pltpu.VMEM((3, spare, lanes), jnp.float32),
                    pltpu.VMEM((1,) + m_block, jnp.float32),
                    pltpu.VMEM((1, depth, spare, lanes), jnp.float32),
                    pltpu.SemaphoreType.DMA((len(sources),)),
                ],
            ),
            out_shape=[f32(s) for s in out_shapes],
            compiler_params=params,
            cost_estimate=cost(steps << 27, 1 << 25),
            name=name,
        )(values, *pieces, *([1.0 / members] if last else []), *sources, band)

    half = groups // 2
    own, next_chunks, t_all = lax.optimization_barrier((own, next_chunks, t_all))
    with jax.named_scope("depth_a"):
        before_a, after_a = neighbours((own[:half], own[:half]), "slab")
    mean_t, var_t = pl.pallas_call(
        template_kernel,
        grid=(clusters,),
        in_specs=[
            pl.BlockSpec((1,) + t_block, lambda i, k=k: (k * clusters + i, 0, 0, 0)) for k in range(3)
        ]
        + [whole(band.shape)],
        out_specs=[block(m_block)] * 2,
        out_shape=[f32((clusters,) + m_block)] * 2,
        scratch_shapes=[
            pltpu.VMEM((2, middle_depth, spare, lanes), jnp.float32),
            pltpu.VMEM((2, spare, lanes), jnp.float32),
        ],
        compiler_params=params,
        cost_estimate=cost(1 << 28, 1 << 23),
        name="templates",
    )(t_all, t_all, t_all, band)

    own, next_chunks, before_a, after_a, mean_t = lax.optimization_barrier(
        (own, next_chunks, before_a, after_a, mean_t)
    )
    with jax.named_scope("swap_1"):
        next_own = exchange(next_chunks)
    with jax.named_scope("depth_b"):
        before_b, after_b = neighbours((own[half:], own[half:]), "slab")
    first_labels = own_labels[:, 0]
    rim_index = index[:half]
    sums = slots_call(
        "slots_a",
        half,
        table(rim_index, rim_index, first_labels[:half], half),
        (before_a, own, after_a),
        (),
        False,
    )
    sums = slots_call(
        "slots_b",
        half,
        table(rim_index + half, rim_index, first_labels[half:], half),
        (before_b, own, after_b),
        sums,
        False,
    )
    next_own, *sums = lax.optimization_barrier((next_own, *sums))

    def finish(steps):
        def branch():
            values = table(order[:steps], place[:steps], labels_in_order[:steps], live_count)
            picked = pl.pallas_call(
                pick_kernel,
                grid_spec=pltpu.PrefetchScalarGridSpec(
                    num_scalar_prefetch=1,
                    grid=(steps,),
                    in_specs=[in_order(t_block, 0)],
                    out_specs=pl.BlockSpec((1,) + t_block, lambda i, values: (i, 0, 0, 0)),
                ),
                out_shape=f32((steps,) + t_block),
                compiler_params=params,
                cost_estimate=cost(1 << 20, steps << 20),
                name="pick",
            )(values, next_own)
            with jax.named_scope("depth_c"):
                next_before, next_after = neighbours((picked, picked), "slab")
            pieces = (next_before, next_own, next_after)
            return slots_call("slots_c", steps, values, pieces, sums, True)[0]

        return branch

    sizes = (2, 4, groups)
    which = sum((live_count > size).astype(jnp.int32) for size in sizes[:-1])
    return lax.switch(which, [finish(size) for size in sizes])


def solution(mesh):
    in_specs = (P("subj", "slab", None, None), P(None, "slab", "subj", None), P(), P())
    out_specs = P(None, "slab", "subj", None)
    return jax.shard_map(
        per_device, mesh=mesh, in_specs=in_specs, out_specs=out_specs, check_vma=False
    )
```

```python
import functools

import jax
import jax.numpy as jnp
from jax import lax
from jax.experimental import pallas as pl
from jax.experimental.pallas import tpu as pltpu
from jax.sharding import PartitionSpec as P


RADIUS = 4
RIM = 2 * RADIUS
WINDOW = 2 * RADIUS + 1
INVERSE = 1.0 / float(WINDOW**3)
ROWS = 8
epsilon = 1e-05


def neighbours(block, axis):
    low, high = block
    count = lax.axis_size(axis)
    forward = [(i, i + 1) for i in range(count - 1)]
    backward = [(target, source) for source, target in forward]
    return lax.ppermute(high, axis, forward), lax.ppermute(low, axis, backward)


def window(planes):
    count = len(planes)
    outputs = count - WINDOW + 1
    prefix, suffix = list(planes), list(planes)
    for i in range(count):
        if i % WINDOW:
            prefix[i] = prefix[i - 1] + planes[i]
    for i in reversed(range(min(outputs - outputs % WINDOW + WINDOW, count) - 1)):
        if i % WINDOW == 0 and i + WINDOW <= count:
            suffix[i] = prefix[i + WINDOW - 1]
        elif i % WINDOW < WINDOW - 1:
            suffix[i] = suffix[i + 1] + planes[i]
    return [
        suffix[i] if i % WINDOW == 0 else suffix[i] + prefix[i + WINDOW - 1]
        for i in range(outputs)
    ]


def y_box(values, band_ref):
    high = values.astype(jnp.bfloat16)
    rest = (values - high.astype(jnp.float32)).astype(jnp.bfloat16)
    return jnp.dot(
        jnp.concatenate([high, rest], axis=1), band_ref[...], preferred_element_type=jnp.float32
    )


def zy_box(channels, columns, band_ref, out_ref, unroll):
    while columns % unroll:
        unroll -= 1

    def step(i, carry):
        sums, places = [], []
        for j in range(unroll):
            rows = pl.ds(pl.multiple_of((i * unroll + j) * ROWS, ROWS), ROWS)
            for c, planes in enumerate(channels(rows)):
                boxes = window(planes)
                sums += boxes
                places += [(c, z, rows) for z in range(len(boxes))]
        boxed = y_box(jnp.concatenate(sums, axis=0), band_ref)
        for k, (c, z, rows) in enumerate(places):
            out_ref[c, z, rows, :] = boxed[k * ROWS : (k + 1) * ROWS]
        return carry

    lax.fori_loop(0, columns // unroll, step, 0)


def x_box(ref, c, z, count, work, slot):
    third = RADIUS - 1
    wide = count + 2 * RADIUS
    work[slot, :wide] = sum_of([ref[c, z, pl.ds(d, wide), :] for d in range(third)])
    return sum_of([work[slot, pl.ds(d * third, count), :] for d in range(third)])


def sum_of(values):
    return functools.reduce(lambda a, b: a + b, values)


def layers(refs, index, rows):
    depth = refs[0].shape[1]
    return [ref[index, z, rows, :] for ref in refs for z in range(depth)]


def template_kernel(before, own, after, band, mean_ref, var_ref, work, thirds):
    def channels(rows):
        planes = layers((before, own, after), 0, rows)
        return planes, [v * v for v in planes]

    zy_box(channels, own.shape[2] // ROWS, band, work, 9)

    def step(z, carry):
        count = mean_ref.shape[2]
        total = x_box(work, 0, z, count, thirds, 0)
        mean = total * INVERSE
        mean_ref[0, z] = mean
        var_ref[0, z] = x_box(work, 1, z, count, thirds, 1) - total * mean
        return carry

    lax.fori_loop(0, mean_ref.shape[1], step, 0, unroll=8)


def clear_rim(ref, index, edges):
    depth, width = ref.shape[1], ref.shape[2]
    parts = (
        (slice(None), slice(0, RADIUS)),
        (slice(None), slice(width - RADIUS, width)),
        (slice(0, RADIUS), slice(None)),
        (slice(depth - RADIUS, depth), slice(None)),
    )
    for edge, (z, x) in zip(edges, parts):

        @pl.when(edge != 0)
        def _():
            part = ref[index, z, x, :]
            ref[index, z, x, :] = jnp.zeros_like(part)


def order_kernel(slots, clusters, labels, counts, table):
    groups, total = counts.shape[0], labels.shape[0]
    members = [jnp.int32(0) for _ in range(clusters)]
    place = jnp.int32(0)
    for i in range(2 * total):
        table[i] = jnp.int32(0)
    for j in range(slots):
        for g in range(groups):
            slot = g * slots + j
            label = labels[slot]
            live = (j < counts[g]).astype(jnp.int32)
            table[place] = jnp.int32(slot)
            table[total + place] = label
            members = [m + live * (label == k).astype(jnp.int32) for k, m in enumerate(members)]
            place = place + live
    table[2 * total] = place
    edges = [
        lax.axis_index("subj") == 0,
        lax.axis_index("subj") == lax.axis_size("subj") - 1,
        lax.axis_index("slab") == 0,
        lax.axis_index("slab") == lax.axis_size("slab") - 1,
    ]
    for i, edge in enumerate(edges):
        table[2 * total + 1 + i] = edge.astype(jnp.int32)
    for k in range(clusters):
        table[2 * total + 5 + k] = members[k]


def pick_kernel(base, total, scalars, source, out_ref, held, read_sems, write_sems):
    count = held.shape[0]
    reads = [
        pltpu.make_async_copy(
            source.at[scalars[jnp.minimum(base + i, scalars[2 * total] - 1)]],
            held.at[i],
            read_sems.at[i],
        )
        for i in range(count)
    ]
    writes = [
        pltpu.make_async_copy(held.at[i], out_ref.at[i], write_sems.at[i]) for i in range(count)
    ]
    for read in reads:
        read.start()
    for read, write in zip(reads, writes):
        read.wait()
        write.start()
    for write in writes:
        write.wait()


def chunk_kernel(source, out_ref):
    count, padded = out_ref.shape[0], out_ref.shape[3]
    extent = padded - 2 * RIM
    length = source.shape[2]
    for g in range(count):
        low = max(g * extent - RIM, 0)
        high = min(g * extent + extent + RIM, length)
        start = low - (g * extent - RIM)
        stop = start + high - low
        out_ref[g, 0, :, start:stop, :] = source[0, :, low:high, :]
        for edge in (slice(0, start), slice(stop, padded)):
            if edge.stop > edge.start:
                out_ref[g, 0, :, edge, :] = jnp.zeros_like(out_ref[g, 0, :, edge, :])


def slot_kernel(first, last, base, total, scalars, before, own, after, *rest):
    count = 5 if first else 8
    sources, rest = rest[:count], rest[count:]
    band, *rest = rest
    if last:
        out_ref, *rest = rest
        targets, rest = rest[:8], rest[8:]
        sum_a, sum_q, sum_p = targets[5:]
    else:
        sum_a, sum_q, sum_p, *rest = rest
        targets, rest = list(rest[:5]) + ([] if first else [sum_a, sum_q, sum_p]), rest[5:]
    t_before, t_own, t_after, mean_t, var_t = targets[:5]
    work, thirds, coef, boxed, sems = rest
    step_index = pl.program_id(0)
    live_count = scalars[2 * total] - base
    edges = [scalars[2 * total + 1 + i] for i in range(4)]
    label = scalars[total + jnp.minimum(base + step_index, total - 1)]
    copies = [
        pltpu.make_async_copy(source, target, sems.at[i])
        for i, (source, target) in enumerate(zip(sources, targets))
    ]

    @pl.when(step_index == 0)
    def _():
        for copy in copies:
            copy.start()
        if first:
            for ref in (sum_a, sum_q, sum_p):
                ref[...] = jnp.zeros_like(ref)
        for copy in copies[:3]:
            copy.wait()

    @pl.when(step_index < live_count)
    def _():
        def channels(rows):
            s = layers((before, own, after), 0, rows)
            t = layers((t_before, t_own, t_after), label, rows)
            return s, [v * v for v in s], [v * w for v, w in zip(s, t)]

        zy_box(channels, own.shape[2] // ROWS, band, work, 9)

    @pl.when(step_index == 0)
    def _():
        for copy in copies[3:]:
            copy.wait()

    @pl.when(step_index < live_count)
    def _():
        width = coef.shape[2]

        def middle(z, carry):
            s_sum = x_box(work, 0, z, width, thirds, 0)
            s_var = x_box(work, 1, z, width, thirds, 1) - s_sum * (s_sum * INVERSE)
            t_mean = mean_t[label, z]
            covariance = x_box(work, 2, z, width, thirds, 2) - s_sum * t_mean
            weight = covariance / (s_var * var_t[label, z] + epsilon)
            spread = weight * s_var
            coef[0, z] = weight
            sum_a[label, z] += weight * (s_sum * INVERSE - spread * t_mean)
            sum_q[label, z] += weight * spread
            return carry

        lax.fori_loop(0, coef.shape[1], middle, 0, unroll=8)
        clear_rim(coef, 0, edges)

        def weights(rows):
            return ([coef[0, z, rows, :] for z in range(coef.shape[1])],)

        zy_box(weights, width // ROWS, band, boxed, 8)

        def close(z, carry):
            centre = own[0, z, RIM : own.shape[2] - RIM, :]
            sum_p[label, z] += x_box(boxed, 0, z, sum_p.shape[2], thirds, 0) * centre
            return carry

        lax.fori_loop(0, sum_p.shape[1], close, 0, unroll=8)

    if not last:
        return

    @pl.when(step_index == pl.num_programs(0) - 1)
    def _():
        def cluster(k, carry):
            member_count = scalars[2 * total + 5 + k].astype(jnp.float32)
            scale = 1.0 / jnp.full((1, out_ref.shape[3]), member_count)
            clear_rim(sum_a, k, edges)
            clear_rim(sum_q, k, edges)

            def channels(rows):
                return [[ref[k, z, rows, :] for z in range(ref.shape[1])] for ref in (sum_a, sum_q)]

            zy_box(channels, sum_a.shape[2] // ROWS, band, work, 8)

            def step(z, carry):
                t = t_own[k, z, RIM : t_own.shape[2] - RIM, :]
                width = out_ref.shape[2]
                gradient = sum_p[k, z] - x_box(work, 0, z, width, thirds, 0)
                gradient = gradient - x_box(work, 1, z, width, thirds, 1) * t
                out_ref[k, z] = t + gradient * scale
                return carry

            return lax.fori_loop(0, out_ref.shape[1], step, carry, unroll=8)

        lax.fori_loop(0, out_ref.shape[0], cluster, 0)


def per_device(subjects, templates, labels, group_live_counts):
    slots, depth, length, lanes = subjects.shape
    clusters, _, extent, _ = templates.shape
    groups = group_live_counts.shape[0]
    padded = extent + 2 * RIM
    middle_depth, middle_extent = depth + RIM, extent + RIM

    reach = jnp.abs(jnp.arange(lanes)[:, None] - jnp.arange(lanes)[None, :]) <= RADIUS
    band = jnp.concatenate([reach, reach], axis=0).astype(jnp.bfloat16)

    def block(shape):
        return pl.BlockSpec((1,) + shape, lambda i, *_: (i,) + (0,) * len(shape))

    def whole(shape):
        return pl.BlockSpec(shape, lambda i, *_: (0,) * len(shape), pipeline_mode=pl.Buffered(1))

    t_block = (depth, padded, lanes)
    m_block = (middle_depth, middle_extent, lanes)
    o_block = (depth, extent, lanes)
    spare = padded + ROWS
    f32 = functools.partial(jax.ShapeDtypeStruct, dtype=jnp.float32)
    params = pltpu.CompilerParams(vmem_limit_bytes=60 * 1024 * 1024)

    def cost(count, size):
        return pl.CostEstimate(flops=count, bytes_accessed=size, transcendentals=0)

    piece = 4 if depth % 4 == 0 else depth

    def exchange(chunks):
        return lax.all_to_all(chunks, "subj", 0, 0, tiled=True)

    low, high = neighbours((templates[:, :, :RIM], templates[:, :, extent - RIM :]), "subj")
    t_own = jnp.concatenate([low, templates, high], axis=2)
    part = groups - groups // 2 + 1
    room = groups // 2
    final = groups - part + room
    total = groups * slots
    in_smem = pl.BlockSpec(memory_space=pltpu.SMEM)
    table = pl.pallas_call(
        functools.partial(order_kernel, slots, clusters),
        in_specs=[in_smem] * 2,
        out_specs=in_smem,
        out_shape=jax.ShapeDtypeStruct((2 * total + 5 + clusters,), jnp.int32),
        name="order",
    )(labels, group_live_counts)
    crowded = jnp.sum(group_live_counts) > part + final

    volumes, t_own = lax.optimization_barrier((subjects, t_own))
    t_before, t_after = neighbours((t_own, t_own), "slab")
    chunks = pl.pallas_call(
        chunk_kernel,
        grid=(slots, depth // piece),
        in_specs=[pl.BlockSpec((1, piece, length, lanes), lambda j, z: (j, z, 0, 0))],
        out_specs=pl.BlockSpec((groups, 1, piece, padded, lanes), lambda j, z: (0, j, z, 0, 0)),
        out_shape=f32((groups, slots) + t_block),
        compiler_params=params,
        cost_estimate=cost(1 << 20, 1 << 23),
        name="chunks",
    )(volumes)
    chunks, band, table = lax.optimization_barrier((chunks, band, table))
    own = exchange(chunks)

    sum_shapes = [(clusters,) + m_block] * 2 + [(clusters,) + o_block]
    anywhere = pl.BlockSpec(memory_space=pl.ANY)

    def slots_call(base, steps, pieces, sums, last):
        first = not sums
        sources = [t_before, t_own, t_after, mean_t, var_t, *sums]
        out_shapes = [(clusters,) + o_block] if last else sum_shapes
        scratch = sources if last else sources[:5]

        def of_slot(i, values):
            return (values[jnp.minimum(base + i, values[2 * total] - 1)], 0, 0, 0)

        def of_step(i, values):
            return (jnp.maximum(jnp.minimum(i, values[2 * total] - 1 - base), 0), 0, 0, 0)

        blocks = [pl.BlockSpec((1,) + t_block, chosen) for chosen in (of_step, of_slot, of_step)]
        return pl.pallas_call(
            functools.partial(slot_kernel, first, last, base, total),
            grid_spec=pltpu.PrefetchScalarGridSpec(
                num_scalar_prefetch=1,
                grid=(steps,),
                in_specs=blocks + [anywhere] * len(sources) + [whole(band.shape)],
                out_specs=[whole(s) for s in out_shapes],
                scratch_shapes=[pltpu.VMEM(s.shape, jnp.float32) for s in scratch]
                + [
                    pltpu.VMEM((3, middle_depth, spare, lanes), jnp.float32),
                    pltpu.VMEM((3, spare, lanes), jnp.float32),
                    pltpu.VMEM((1,) + m_block, jnp.float32),
                    pltpu.VMEM((1, depth, spare, lanes), jnp.float32),
                    pltpu.SemaphoreType.DMA((len(sources),)),
                ],
            ),
            out_shape=[f32(s) for s in out_shapes],
            compiler_params=params,
            cost_estimate=cost(steps << 27, 1 << 25),
        )(table, *pieces, *sources, band)

    def pick(base, steps):
        return pl.pallas_call(
            functools.partial(pick_kernel, base, total),
            in_specs=[in_smem, anywhere],
            out_specs=anywhere,
            out_shape=f32((steps,) + t_block),
            scratch_shapes=[
                pltpu.VMEM((steps,) + t_block, jnp.float32),
                pltpu.SemaphoreType.DMA((steps,)),
                pltpu.SemaphoreType.DMA((steps,)),
            ],
            compiler_params=params,
            cost_estimate=cost(1 << 20, 1 << 22),
        )(table, own)

    own = own.reshape((groups * slots,) + t_block)
    picked = pick(0, part)
    before, after = neighbours((picked, picked), "slab")
    final_picked = pick(part, final)
    final_before, final_after = neighbours((final_picked, final_picked), "slab")
    own, t_before, t_after = lax.optimization_barrier((own, t_before, t_after))
    mean_t, var_t = pl.pallas_call(
        template_kernel,
        grid=(clusters,),
        in_specs=[block(t_block)] * 3 + [whole(band.shape)],
        out_specs=[block(m_block)] * 2,
        out_shape=[f32((clusters,) + m_block)] * 2,
        scratch_shapes=[
            pltpu.VMEM((2, middle_depth, spare, lanes), jnp.float32),
            pltpu.VMEM((2, spare, lanes), jnp.float32),
        ],
        compiler_params=params,
        cost_estimate=cost(1 << 28, 1 << 23),
        name="templates",
    )(t_before, t_own, t_after, band)

    sums = slots_call(0, part, (before, own, after), (), False)
    pieces = (final_before, own, final_after)

    def all_fit():
        return slots_call(part, final, pieces, sums, True)[0]

    def more():
        others = pick(groups + room, groups - room)
        last_before, last_after = neighbours((others, others), "slab")
        partial = slots_call(part, final, pieces, sums, False)
        last_pieces = (last_before, own, last_after)
        return slots_call(groups + room, groups - room, last_pieces, partial, True)[0]

    return lax.cond(crowded, more, all_fit)


def solution(mesh):
    in_specs = (P("subj", "slab", None, None), P(None, "slab", "subj", None), P(), P())
    out_specs = P(None, "slab", "subj", None)
    return jax.shard_map(
        per_device, mesh=mesh, in_specs=in_specs, out_specs=out_specs, check_vma=False
    )
```

```python
import functools

import jax
import jax.numpy as jnp
from jax import lax
from jax.experimental import pallas as pl
from jax.experimental.pallas import tpu as pltpu
from jax.sharding import PartitionSpec as P


RADIUS = 4
RIM = 2 * RADIUS
WINDOW = 2 * RADIUS + 1
INVERSE = 1.0 / float(WINDOW**3)
ROWS = 8
epsilon = 1e-05


def neighbours(block, axis):
    low, high = block
    count = lax.axis_size(axis)
    forward = [(i, i + 1) for i in range(count - 1)]
    backward = [(target, source) for source, target in forward]
    return lax.ppermute(high, axis, forward), lax.ppermute(low, axis, backward)


def window(planes):
    count = len(planes)
    outputs = count - WINDOW + 1
    prefix, suffix = list(planes), list(planes)
    for i in range(count):
        if i % WINDOW:
            prefix[i] = prefix[i - 1] + planes[i]
    for i in reversed(range(min(outputs - outputs % WINDOW + WINDOW, count) - 1)):
        if i % WINDOW == 0 and i + WINDOW <= count:
            suffix[i] = prefix[i + WINDOW - 1]
        elif i % WINDOW < WINDOW - 1:
            suffix[i] = suffix[i + 1] + planes[i]
    return [
        suffix[i] if i % WINDOW == 0 else suffix[i] + prefix[i + WINDOW - 1]
        for i in range(outputs)
    ]


def y_box(values, band_ref):
    high = values.astype(jnp.bfloat16)
    rest = (values - high.astype(jnp.float32)).astype(jnp.bfloat16)
    return jnp.dot(
        jnp.concatenate([high, rest], axis=1), band_ref[...], preferred_element_type=jnp.float32
    )


def zy_box(channels, columns, band_ref, out_ref, unroll):
    while columns % unroll:
        unroll -= 1

    def step(i, carry):
        sums, places = [], []
        for j in range(unroll):
            rows = pl.ds(pl.multiple_of((i * unroll + j) * ROWS, ROWS), ROWS)
            for c, planes in enumerate(channels(rows)):
                boxes = window(planes)
                sums += boxes
                places += [(c, z, rows) for z in range(len(boxes))]
        boxed = y_box(jnp.concatenate(sums, axis=0), band_ref)
        for k, (c, z, rows) in enumerate(places):
            out_ref[c, z, rows, :] = boxed[k * ROWS : (k + 1) * ROWS]
        return carry

    lax.fori_loop(0, columns // unroll, step, 0)


def x_box(ref, c, z, count, work, slot):
    third = RADIUS - 1
    wide = count + 2 * RADIUS
    work[slot, :wide] = sum_of([ref[c, z, pl.ds(d, wide), :] for d in range(third)])
    return sum_of([work[slot, pl.ds(d * third, count), :] for d in range(third)])


def sum_of(values):
    return functools.reduce(lambda a, b: a + b, values)


def layers(refs, index, rows):
    depth = refs[0].shape[1]
    return [ref[index, z, rows, :] for ref in refs for z in range(depth)]


def template_kernel(before, own, after, band, mean_ref, var_ref, work, thirds):
    def channels(rows):
        planes = layers((before, own, after), 0, rows)
        return planes, [v * v for v in planes]

    zy_box(channels, own.shape[2] // ROWS, band, work, 9)

    def step(z, carry):
        count = mean_ref.shape[2]
        total = x_box(work, 0, z, count, thirds, 0)
        mean = total * INVERSE
        mean_ref[0, z] = mean
        var_ref[0, z] = x_box(work, 1, z, count, thirds, 1) - total * mean
        return carry

    lax.fori_loop(0, mean_ref.shape[1], step, 0, unroll=8)


def clear_rim(ref, index, edges):
    depth, width = ref.shape[1], ref.shape[2]
    parts = (
        (slice(None), slice(0, RADIUS)),
        (slice(None), slice(width - RADIUS, width)),
        (slice(0, RADIUS), slice(None)),
        (slice(depth - RADIUS, depth), slice(None)),
    )
    for edge, (z, x) in zip(edges, parts):

        @pl.when(edge != 0)
        def _():
            part = ref[index, z, x, :]
            ref[index, z, x, :] = jnp.zeros_like(part)


def order_kernel(slots, clusters, labels, counts, table):
    groups, total = counts.shape[0], labels.shape[0]
    members = [jnp.int32(0) for _ in range(clusters)]
    place = jnp.int32(0)
    for i in range(2 * total):
        table[i] = jnp.int32(0)
    for j in range(slots):
        for g in range(groups):
            slot = g * slots + j
            label = labels[slot]
            live = (j < counts[g]).astype(jnp.int32)
            table[place] = jnp.int32(slot)
            table[total + place] = label
            members = [m + live * (label == k).astype(jnp.int32) for k, m in enumerate(members)]
            place = place + live
    table[2 * total] = place
    edges = [
        lax.axis_index("subj") == 0,
        lax.axis_index("subj") == lax.axis_size("subj") - 1,
        lax.axis_index("slab") == 0,
        lax.axis_index("slab") == lax.axis_size("slab") - 1,
    ]
    for i, edge in enumerate(edges):
        table[2 * total + 1 + i] = edge.astype(jnp.int32)
    for k in range(clusters):
        table[2 * total + 5 + k] = members[k]


def pick_kernel(base, total, scalars, source, out_ref, held, read_sems, write_sems):
    count = held.shape[0]
    reads = [
        pltpu.make_async_copy(
            source.at[scalars[jnp.minimum(base + i, scalars[2 * total] - 1)]],
            held.at[i],
            read_sems.at[i],
        )
        for i in range(count)
    ]
    writes = [
        pltpu.make_async_copy(held.at[i], out_ref.at[i], write_sems.at[i]) for i in range(count)
    ]
    for read in reads:
        read.start()
    for read, write in zip(reads, writes):
        read.wait()
        write.start()
    for write in writes:
        write.wait()


def chunk_kernel(source, out_ref, held, read_sems, write_sems):
    slots, depth, length, _ = source.shape
    count, padded = out_ref.shape[0], out_ref.shape[3]
    extent = padded - 2 * RIM
    half = depth // 2
    parts = [(j, pl.ds(k * half, half)) for j in range(slots) for k in range(2)]
    reads = [
        pltpu.make_async_copy(
            source.at[j, z], held.at[j, z, pl.ds(RIM, length), :], read_sems.at[i]
        )
        for i, (j, z) in enumerate(parts)
    ]
    for read in reads:
        read.start()
    edge = jnp.zeros((slots, depth, RIM, held.shape[3]), jnp.float32)
    held[:, :, :RIM, :] = edge
    held[:, :, RIM + length :, :] = edge
    writes = []
    for i, (j, z) in enumerate(parts):
        reads[i].wait()
        for g in range(count):
            write = pltpu.make_async_copy(
                held.at[j, z, pl.ds(g * extent, padded), :],
                out_ref.at[g, j, z],
                write_sems.at[i * count + g],
            )
            write.start()
            writes.append(write)
    for write in writes:
        write.wait()


def slot_kernel(first, last, base, total, scalars, before, own, after, *rest):
    count = 5 if first else 8
    sources, rest = rest[:count], rest[count:]
    band, *rest = rest
    if last:
        out_ref, *rest = rest
        targets, rest = rest[:8], rest[8:]
        sum_a, sum_q, sum_p = targets[5:]
    else:
        sum_a, sum_q, sum_p, *rest = rest
        targets, rest = list(rest[:5]) + ([] if first else [sum_a, sum_q, sum_p]), rest[5:]
    t_before, t_own, t_after, mean_t, var_t = targets[:5]
    work, thirds, coef, boxed, sems = rest
    step_index = pl.program_id(0)
    live_count = scalars[2 * total] - base
    edges = [scalars[2 * total + 1 + i] for i in range(4)]
    label = scalars[total + jnp.minimum(base + step_index, total - 1)]
    copies = [
        pltpu.make_async_copy(source, target, sems.at[i])
        for i, (source, target) in enumerate(zip(sources, targets))
    ]

    @pl.when(step_index == 0)
    def _():
        for copy in copies:
            copy.start()
        if first:
            for ref in (sum_a, sum_q, sum_p):
                ref[...] = jnp.zeros_like(ref)
        for copy in copies[:3]:
            copy.wait()

    @pl.when(step_index < live_count)
    def _():
        def channels(rows):
            s = layers((before, own, after), 0, rows)
            t = layers((t_before, t_own, t_after), label, rows)
            return s, [v * v for v in s], [v * w for v, w in zip(s, t)]

        zy_box(channels, own.shape[2] // ROWS, band, work, 9)

    @pl.when(step_index == 0)
    def _():
        for copy in copies[3:]:
            copy.wait()

    @pl.when(step_index < live_count)
    def _():
        width = coef.shape[2]

        def middle(z, carry):
            s_sum = x_box(work, 0, z, width, thirds, 0)
            s_var = x_box(work, 1, z, width, thirds, 1) - s_sum * (s_sum * INVERSE)
            t_mean = mean_t[label, z]
            covariance = x_box(work, 2, z, width, thirds, 2) - s_sum * t_mean
            weight = covariance / (s_var * var_t[label, z] + epsilon)
            spread = weight * s_var
            coef[0, z] = weight
            sum_a[label, z] += weight * (s_sum * INVERSE - spread * t_mean)
            sum_q[label, z] += weight * spread
            return carry

        lax.fori_loop(0, coef.shape[1], middle, 0, unroll=8)
        clear_rim(coef, 0, edges)

        def weights(rows):
            return ([coef[0, z, rows, :] for z in range(coef.shape[1])],)

        zy_box(weights, width // ROWS, band, boxed, 8)

        def close(z, carry):
            centre = own[0, z, RIM : own.shape[2] - RIM, :]
            sum_p[label, z] += x_box(boxed, 0, z, sum_p.shape[2], thirds, 0) * centre
            return carry

        lax.fori_loop(0, sum_p.shape[1], close, 0, unroll=8)

    if not last:
        return

    @pl.when(step_index == pl.num_programs(0) - 1)
    def _():
        def cluster(k, carry):
            member_count = scalars[2 * total + 5 + k].astype(jnp.float32)
            scale = 1.0 / jnp.full((1, out_ref.shape[3]), member_count)
            clear_rim(sum_a, k, edges)
            clear_rim(sum_q, k, edges)

            def channels(rows):
                return [[ref[k, z, rows, :] for z in range(ref.shape[1])] for ref in (sum_a, sum_q)]

            zy_box(channels, sum_a.shape[2] // ROWS, band, work, 8)

            def step(z, carry):
                t = t_own[k, z, RIM : t_own.shape[2] - RIM, :]
                width = out_ref.shape[2]
                gradient = sum_p[k, z] - x_box(work, 0, z, width, thirds, 0)
                gradient = gradient - x_box(work, 1, z, width, thirds, 1) * t
                out_ref[k, z] = t + gradient * scale
                return carry

            return lax.fori_loop(0, out_ref.shape[1], step, carry, unroll=8)

        lax.fori_loop(0, out_ref.shape[0], cluster, 0)


def per_device(subjects, templates, labels, group_live_counts):
    slots, depth, length, lanes = subjects.shape
    clusters, _, extent, _ = templates.shape
    groups = group_live_counts.shape[0]
    padded = extent + 2 * RIM
    middle_depth, middle_extent = depth + RIM, extent + RIM

    reach = jnp.abs(jnp.arange(lanes)[:, None] - jnp.arange(lanes)[None, :]) <= RADIUS
    band = jnp.concatenate([reach, reach], axis=0).astype(jnp.bfloat16)

    def block(shape):
        return pl.BlockSpec((1,) + shape, lambda i, *_: (i,) + (0,) * len(shape))

    def whole(shape):
        return pl.BlockSpec(shape, lambda i, *_: (0,) * len(shape), pipeline_mode=pl.Buffered(1))

    t_block = (depth, padded, lanes)
    m_block = (middle_depth, middle_extent, lanes)
    o_block = (depth, extent, lanes)
    spare = padded + ROWS
    f32 = functools.partial(jax.ShapeDtypeStruct, dtype=jnp.float32)
    params = pltpu.CompilerParams(vmem_limit_bytes=60 * 1024 * 1024)

    def cost(count, size):
        return pl.CostEstimate(flops=count, bytes_accessed=size, transcendentals=0)

    def exchange(chunks):
        return lax.all_to_all(chunks, "subj", 0, 0, tiled=True)

    low, high = neighbours((templates[:, :, :RIM], templates[:, :, extent - RIM :]), "subj")
    t_own = jnp.concatenate([low, templates, high], axis=2)
    part = groups - groups // 4
    total = groups * slots
    in_smem = pl.BlockSpec(memory_space=pltpu.SMEM)
    anywhere = pl.BlockSpec(memory_space=pl.ANY)
    table = pl.pallas_call(
        functools.partial(order_kernel, slots, clusters),
        in_specs=[in_smem] * 2,
        out_specs=in_smem,
        out_shape=jax.ShapeDtypeStruct((2 * total + 5 + clusters,), jnp.int32),
        name="order",
    )(labels, group_live_counts)
    extra = jnp.sum(group_live_counts) - groups
    sizes = [size for size in (1, 2, 3, 4) if size < groups] + [groups]
    which = sum((extra > size).astype(jnp.int32) for size in sizes[:-1])

    volumes, t_own = lax.optimization_barrier((subjects, t_own))
    t_before, t_after = neighbours((t_own, t_own), "slab")
    chunks = pl.pallas_call(
        chunk_kernel,
        in_specs=[anywhere],
        out_specs=anywhere,
        scratch_shapes=[
            pltpu.VMEM((slots, depth, length + 2 * RIM, lanes), jnp.float32),
            pltpu.SemaphoreType.DMA((2 * slots,)),
            pltpu.SemaphoreType.DMA((2 * slots * groups,)),
        ],
        out_shape=f32((groups, slots) + t_block),
        compiler_params=params,
        cost_estimate=cost(1 << 20, 1 << 23),
        name="chunks",
    )(volumes)
    chunks, band, table, which = lax.optimization_barrier((chunks, band, table, which))
    own = exchange(chunks)

    sum_shapes = [(clusters,) + m_block] * 2 + [(clusters,) + o_block]

    def slots_call(base, steps, pieces, stats, sums, last):
        first = not sums
        sources = [t_before, t_own, t_after, *stats, *sums]
        out_shapes = [(clusters,) + o_block] if last else sum_shapes
        scratch = sources if last else sources[:5]

        def of_slot(i, values):
            return (values[jnp.minimum(base + i, values[2 * total] - 1)], 0, 0, 0)

        def of_step(i, values):
            return (jnp.maximum(jnp.minimum(i, values[2 * total] - 1 - base), 0), 0, 0, 0)

        blocks = [pl.BlockSpec((1,) + t_block, chosen) for chosen in (of_step, of_slot, of_step)]
        return pl.pallas_call(
            functools.partial(slot_kernel, first, last, base, total),
            grid_spec=pltpu.PrefetchScalarGridSpec(
                num_scalar_prefetch=1,
                grid=(steps,),
                in_specs=blocks + [anywhere] * len(sources) + [whole(band.shape)],
                out_specs=[whole(s) for s in out_shapes],
                scratch_shapes=[pltpu.VMEM(s.shape, jnp.float32) for s in scratch]
                + [
                    pltpu.VMEM((3, middle_depth, spare, lanes), jnp.float32),
                    pltpu.VMEM((3, spare, lanes), jnp.float32),
                    pltpu.VMEM((1,) + m_block, jnp.float32),
                    pltpu.VMEM((1, depth, spare, lanes), jnp.float32),
                    pltpu.SemaphoreType.DMA((len(sources),)),
                ],
            ),
            out_shape=[f32(s) for s in out_shapes],
            compiler_params=params,
            cost_estimate=cost(steps << 27, 1 << 25),
        )(table, *pieces, *sources, band)

    def pick(base, steps):
        return pl.pallas_call(
            functools.partial(pick_kernel, base, total),
            in_specs=[in_smem, anywhere],
            out_specs=anywhere,
            out_shape=f32((steps,) + t_block),
            scratch_shapes=[
                pltpu.VMEM((steps,) + t_block, jnp.float32),
                pltpu.SemaphoreType.DMA((steps,)),
                pltpu.SemaphoreType.DMA((steps,)),
            ],
            compiler_params=params,
            cost_estimate=cost(1 << 20, 1 << 22),
        )(table, own)

    own = own.reshape((groups * slots,) + t_block)
    own, which = lax.optimization_barrier((own, which))

    def template_sums(t_before, t_after):
        return pl.pallas_call(
            template_kernel,
            grid=(clusters,),
            in_specs=[block(t_block)] * 3 + [whole(band.shape)],
            out_specs=[block(m_block)] * 2,
            out_shape=[f32((clusters,) + m_block)] * 2,
            scratch_shapes=[
                pltpu.VMEM((2, middle_depth, spare, lanes), jnp.float32),
                pltpu.VMEM((2, spare, lanes), jnp.float32),
            ],
            compiler_params=params,
            cost_estimate=cost(1 << 28, 1 << 23),
            name="templates",
        )(t_before, t_own, t_after, band)

    picked = pick(0, part)

    def finish(size):
        final = groups - part + size

        def branch():
            before, after = neighbours((picked, picked), "slab")
            final_picked = pick(part, final)
            stats = template_sums(t_before, t_after)
            final_picked, *stats = lax.optimization_barrier((final_picked, *stats))
            final_before, final_after = neighbours((final_picked, final_picked), "slab")
            sums = slots_call(0, part, (before, own, after), stats, (), False)
            pieces = (final_before, own, final_after)
            return slots_call(part, final, pieces, stats, sums, True)[0]

        return branch

    return lax.switch(which, [finish(size) for size in sizes])


def solution(mesh):
    in_specs = (P("subj", "slab", None, None), P(None, "slab", "subj", None), P(), P())
    out_specs = P(None, "slab", "subj", None)
    return jax.shard_map(
        per_device, mesh=mesh, in_specs=in_specs, out_specs=out_specs, check_vma=False
    )
```
